32 devices in a mesh: rep: 4 (over z), dp: 2 (over x), ctx: 4 (over y, core).
Axes of the slice: x: 2, y: 2, z: 4, core: 2. Of those that a mesh axis runs over, the one named last changes fastest.
Arguments:
- hidden_in: bfloat16 [8, 2048, 2048], P(('rep', 'dp'), 'ctx'), may hold values from -6 to 6
- segments: int32 [8, 2048], P(('rep', 'dp'), 'ctx'), may hold values from -1 to 31, as said below
- cotangent: bfloat16 [8, 2048, 2048], P(('rep', 'dp'), 'ctx'), may hold values from -6 to 6
- attn_gain: float32 [2048], P(('dp', 'ctx')), may hold values from 0.25 to 1.75
- w_query: float32 [2048, 2048], P(('dp', 'ctx')), may hold values from -0.125 to 0.125
- key_projection: float32 [2048, 1024], P(('dp', 'ctx')), may hold values from -0.125 to 0.125
- value_projection: float32 [2048, 1024], P(('dp', 'ctx')), may hold values from -0.125 to 0.125
- q_gain: float32 [128], P(('dp', 'ctx')), may hold values from 1 to 2.5
- k_gain: float32 [128], P(('dp', 'ctx')), may hold values from 0.25 to 1.75
- w_gate: float32 [2048, 16], P(('dp', 'ctx')), may hold values from -0.25 to 0.25
- w_out: float32 [2048, 2048], P(('dp', 'ctx')), may hold values from -1 to 1
- mlp_gain: float32 [2048], P(('dp', 'ctx')), may hold values from 0.25 to 1.75
- w_gate_ff: float32 [2048, 6144], P(('dp', 'ctx')), may hold values from -0.125 to 0.125
- w_up: float32 [2048, 6144], P(('dp', 'ctx')), may hold values from -0.125 to 0.125
- w_down: float32 [6144, 2048], P(('dp', 'ctx')), may hold values from -0.078125 to 0.078125
Outputs:
- layer_out: bfloat16 [8, 2048, 2048], P(('rep', 'dp'), 'ctx')
- input_grad: bfloat16 [8, 2048, 2048], P(('rep', 'dp'), 'ctx')
- grad_attn_gain: float32 [2048], P(('dp', 'ctx'))
- grad_query: float32 [2048, 2048], P(('dp', 'ctx'))
- grad_key: float32 [2048, 1024], P(('dp', 'ctx'))
- grad_value: float32 [2048, 1024], P(('dp', 'ctx'))
- grad_q_gain: float32 [128], P(('dp', 'ctx'))
- grad_k_gain: float32 [128], P(('dp', 'ctx'))
- grad_gate: float32 [2048, 16], P(('dp', 'ctx'))
- grad_out: float32 [2048, 2048], P(('dp', 'ctx'))
- grad_mlp_gain: float32 [2048], P(('dp', 'ctx'))
- grad_gate_ff: float32 [2048, 6144], P(('dp', 'ctx'))
- grad_up: float32 [2048, 6144], P(('dp', 'ctx'))
- grad_down: float32 [6144, 2048], P(('dp', 'ctx'))
The draws below stay inside these ranges and needn't reach their ends.
Inputs may be any that keep to these rules, and one draw needn't show every extreme that they name: `segments`: in each sequence the ids number its 32 documents from 0 at the first token and rise by one at each document's start until the padding; the first document holds at least 768 tokens; every sequence ends with 1 to 256 padding tokens marked -1.
All inputs are finite; a program needn't handle non-finite values.
Results may differ from the reference program's by a relative error of at most 0.02.
The reference program's roundings to bfloat16 on the way count: a program that leaves them out, or rounds other values in their place, can miss the bound.
Values may be sent and summed in bfloat16 or wider, within the bound.
No kernel may reach another device: no remote copies, remote signals or barrier semaphores. Data moves between devices by JAX's collectives and lax.ppermute only.
A program may use at most 448 MiB of HBM per device.

```python
import math
import jax
import jax.numpy as jnp
from jax import lax

MODEL_WIDTH = 2048
QUERY_HEADS = 16
KEY_VALUE_HEADS = 8
HEAD_SIZE = 128
FF = 6144
LEN = 2048
NDOC = 32
SEQS = 8


def draw_segments(key, part):
    score_key, shape_key, pad_key = jax.random.split(jax.random.fold_in(key, 7), 3)
    head = LEN * 3 // 8
    span = LEN - LEN // 8 - head
    raw = jax.random.randint(score_key, (SEQS, span), 0, 1 << 20)
    squared = jax.random.randint(shape_key, (SEQS, 1), 0, 2)
    scores = jnp.where(squared > 0, (raw >> 10) * (raw >> 10), raw)
    scores = scores * span + jnp.arange(span)[None, :]
    chosen = jnp.argsort(scores, axis=1, stable=True)[:, :NDOC - 1]
    marks = jnp.zeros((SEQS, span), jnp.int32)
    rows = jnp.arange(SEQS)[:, None] + jnp.zeros((1, NDOC - 1), jnp.int32)
    marks = marks.at[rows, chosen].set(1)
    starts = jnp.concatenate([jnp.zeros((SEQS, head), jnp.int32), marks, jnp.zeros((SEQS, LEN - head - span), jnp.int32)], axis=1)
    labels = jnp.cumsum(starts, axis=1)
    position = jnp.arange(LEN)[None, :]
    padding = jax.random.randint(pad_key, (SEQS, 1), 1, LEN // 8 + 1)
    return jnp.where(position >= LEN - padding, -1, labels).astype(jnp.int32)


def levels(stream_key, extent, cuts, least, largest):
    level, own = 1.0, jax.random.fold_in(stream_key, 6)
    for axis_at, shards_of in cuts:
        heights = jnp.exp(jax.random.uniform(jax.random.fold_in(own, axis_at), (shards_of,), jnp.float32, least / len(cuts), largest / len(cuts)))
        level = level * jnp.repeat(heights, extent[axis_at] // shards_of).reshape([-1 if axis == axis_at else 1 for axis in range(len(extent))])
    return level


def bell_draw(rng, dims, scale, limit, cuts=(), kind=jnp.bfloat16):
    entries = scale * jax.random.normal(rng, dims, jnp.float32)
    if cuts:
        entries = entries * levels(rng, dims, cuts, -0.22, 0.18)
    return jnp.clip(entries, -limit, limit).astype(kind)


def setup_inputs(seed: int = 0) -> dict:
    arg_keys = jax.random.split(jax.random.key(seed), 16)
    hidden_in = bell_draw(arg_keys[0], (SEQS, LEN, MODEL_WIDTH), 1.0, 6.0, ((0, 8), (1, 4)))
    segments = draw_segments(jax.random.fold_in(arg_keys[15], 71), 0)
    cotangent = bell_draw(arg_keys[2], (SEQS, LEN, MODEL_WIDTH), 1.0, 6.0, ((0, 8), (1, 4)))
    attn_gain = jnp.clip(1.0 + 0.15 * jax.random.normal(arg_keys[3], (MODEL_WIDTH,), jnp.float32), 0.25, 1.75)
    w_query = bell_draw(arg_keys[4], (MODEL_WIDTH, QUERY_HEADS * HEAD_SIZE), MODEL_WIDTH ** -0.5, 0.125, ((0, 8),), jnp.float32)
    key_projection = bell_draw(arg_keys[5], (MODEL_WIDTH, KEY_VALUE_HEADS * HEAD_SIZE), MODEL_WIDTH ** -0.5, 0.125, ((0, 8),), jnp.float32)
    value_projection = bell_draw(arg_keys[6], (MODEL_WIDTH, KEY_VALUE_HEADS * HEAD_SIZE), MODEL_WIDTH ** -0.5, 0.125, ((0, 8),), jnp.float32)
    q_gain = jnp.clip(jnp.exp(math.log(2.5) - 0.916290732 * jax.random.uniform(arg_keys[7], (HEAD_SIZE,), jnp.float32) ** levels(arg_keys[7], (HEAD_SIZE,), ((0, 8),), -0.2, 0.2)), 1.0, 2.5)
    k_gain = jnp.clip(1.0 + 0.15 * jax.random.normal(arg_keys[8], (HEAD_SIZE,), jnp.float32), 0.25, 1.75)
    w_gate = bell_draw(arg_keys[9], (MODEL_WIDTH, QUERY_HEADS), (MODEL_WIDTH // 4) ** -0.5, 0.25, ((0, 8),), jnp.float32)
    w_out = bell_draw(arg_keys[10], (QUERY_HEADS * HEAD_SIZE, MODEL_WIDTH), (QUERY_HEADS * HEAD_SIZE // 64) ** -0.5, 1.0, ((0, 8),), jnp.float32)
    mlp_gain = jnp.clip(1.0 + 0.15 * jax.random.normal(arg_keys[11], (MODEL_WIDTH,), jnp.float32), 0.25, 1.75)
    w_gate_ff = bell_draw(arg_keys[12], (MODEL_WIDTH, FF), MODEL_WIDTH ** -0.5, 0.125, ((0, 8),), jnp.float32)
    w_up = bell_draw(arg_keys[13], (MODEL_WIDTH, FF), MODEL_WIDTH ** -0.5, 0.125, ((0, 8),), jnp.float32)
    w_down = bell_draw(arg_keys[14], (FF, MODEL_WIDTH), FF ** -0.5, 0.078125, ((0, 8),), jnp.float32)
    return dict(hidden_in=hidden_in, segments=segments, cotangent=cotangent, attn_gain=attn_gain, w_query=w_query, key_projection=key_projection, value_projection=value_projection, q_gain=q_gain, k_gain=k_gain, w_gate=w_gate, w_out=w_out, mlp_gain=mlp_gain, w_gate_ff=w_gate_ff, w_up=w_up, w_down=w_down)


epsilon = 1e-06
masked_score = -1e+30
highest = lax.Precision.HIGHEST

@jax.custom_vjp
def reduced_precision(v):
    return lax.optimization_barrier(v.astype(jnp.bfloat16)).astype(jnp.float32)

@jax.custom_vjp
def reduced_precision_back(v):
    return v

def low_keep(v):
    return (reduced_precision(v), None)

def low_pass(kept, grad):
    return (grad,)

def back_keep(v):
    return (v, None)

def back_low(kept, grad):
    return (reduced_precision(grad),)
reduced_precision.defvjp(low_keep, low_pass)
reduced_precision_back.defvjp(back_keep, back_low)

def root_normed(value):
    return value * lax.rsqrt(lax.optimization_barrier(jnp.mean(value * value, axis=-1, keepdims=True)) + epsilon)

def precise_product(left, right):
    return jnp.dot(left, right, precision=highest)

def attend(query_norm_layer, key_norm_layer, value_vectors, seg_row):
    length_total = query_norm_layer.shape[0]
    block_runner = min(512, length_total)
    query_group = QUERY_HEADS // KEY_VALUE_HEADS
    scale = HEAD_SIZE ** (-0.5)
    position = jnp.arange(length_total).astype(jnp.int32)

    def per_block(inputs):
        query_block_rows, seg_query, spot_query = inputs
        grouped_queries = query_block_rows.reshape(block_runner, KEY_VALUE_HEADS, query_group, HEAD_SIZE)
        scores = reduced_precision_back(jnp.einsum('bkgd,tkd->kgbt', grouped_queries, key_norm_layer, precision=highest) * scale)
        allowed = (seg_query[:, None] == seg_row[None, :]) & (position[None, :] <= spot_query[:, None]) & (seg_query[:, None] >= 0) | (position[None, :] == spot_query[:, None])
        scores = jnp.where(allowed[None, None], scores, masked_score)
        peak = lax.optimization_barrier(jnp.max(scores, axis=-1, keepdims=True))
        expon = jnp.exp(scores - peak)
        probs = expon / lax.optimization_barrier(jnp.sum(expon, axis=-1, keepdims=True))
        mixed = jnp.einsum('kgbt,tkd->bkgd', reduced_precision(probs), value_vectors, precision=highest)
        return mixed.reshape(block_runner, QUERY_HEADS, HEAD_SIZE)
    blocks = lax.map(jax.checkpoint(per_block), (query_norm_layer.reshape(length_total // block_runner, block_runner, QUERY_HEADS, HEAD_SIZE), seg_row.reshape(length_total // block_runner, block_runner), position.reshape(length_total // block_runner, block_runner)))
    return blocks.reshape(length_total, QUERY_HEADS, HEAD_SIZE)

def layer(x_rows, seg_row, attn_gain, w_query, key_projection, value_projection, q_gain, k_gain, w_gate, w_out, mlp_gain, w_gate_ff, w_up, w_down):
    length_total = x_rows.shape[0]
    gain_a = reduced_precision(attn_gain)
    query_w = reduced_precision(w_query)
    key_matrix = reduced_precision(key_projection)
    value_matrix = reduced_precision(value_projection)
    gain_q = reduced_precision(q_gain)
    key_gain_vector = reduced_precision(k_gain)
    gate_w = reduced_precision(w_gate)
    out_w = reduced_precision(w_out)
    gain_m = reduced_precision(mlp_gain)
    gateff_w = reduced_precision(w_gate_ff)
    up_w = reduced_precision(w_up)
    down_w = reduced_precision(w_down)
    normed_rows = reduced_precision(root_normed(x_rows) * gain_a)
    queries = reduced_precision_back(precise_product(normed_rows, query_w)).reshape(length_total, QUERY_HEADS, HEAD_SIZE)
    unnormed_keys = reduced_precision_back(precise_product(normed_rows, key_matrix)).reshape(length_total, KEY_VALUE_HEADS, HEAD_SIZE)
    value_vectors = reduced_precision_back(reduced_precision(precise_product(normed_rows, value_matrix))).reshape(length_total, KEY_VALUE_HEADS, HEAD_SIZE)
    logits = reduced_precision_back(precise_product(normed_rows, gate_w))
    query_norm_layer = reduced_precision(root_normed(queries) * gain_q)
    key_norm_layer = reduced_precision(root_normed(unnormed_keys) * key_gain_vector)
    mixed = reduced_precision_back(attend(query_norm_layer, key_norm_layer, value_vectors, seg_row))
    gated = reduced_precision(mixed * jax.nn.sigmoid(logits)[:, :, None]).reshape(length_total, QUERY_HEADS * HEAD_SIZE)
    middle = x_rows + reduced_precision_back(precise_product(gated, out_w))
    normed_m = reduced_precision(root_normed(middle) * gain_m)
    gate_ff = reduced_precision_back(precise_product(normed_m, gateff_w))
    up_ff = reduced_precision_back(precise_product(normed_m, up_w))
    hidden = reduced_precision(jax.nn.silu(gate_ff) * up_ff)
    return middle + reduced_precision_back(precise_product(hidden, down_w))

def reference(hidden_in, segments, cotangent, attn_gain, w_query, key_projection, value_projection, q_gain, k_gain, w_gate, w_out, mlp_gain, w_gate_ff, w_up, w_down):
    weights = (attn_gain, w_query, key_projection, value_projection, q_gain, k_gain, w_gate, w_out, mlp_gain, w_gate_ff, w_up, w_down)

    def per_sequence(running, item):
        x_seq, seg_seq, cot_seq = item

        def forward(x_rows, *params):
            return layer(x_rows, seg_seq, *params)
        result, pullback = jax.vjp(forward, x_seq.astype(jnp.float32), *weights)
        masked = cot_seq.astype(jnp.float32) * (seg_seq >= 0).astype(jnp.float32)[:, None]
        grads = pullback(masked)
        running = tuple((acc + grad for acc, grad in zip(running, grads[1:])))
        return (running, (result.astype(jnp.bfloat16), grads[0].astype(jnp.bfloat16)))
    zeros = tuple((jnp.zeros(w.shape, jnp.float32) for w in weights))
    sums, (outputs, input_grads) = lax.scan(per_sequence, zeros, (hidden_in, segments, cotangent))
    return (outputs, input_grads, sums[0], sums[1], sums[2], sums[3], sums[4], sums[5], sums[6], sums[7], sums[8], sums[9], sums[10], sums[11])
```

```python
import jax
import jax.numpy as jnp
from jax import lax
from jax.experimental import pallas as pl
from jax.experimental.pallas import tpu as pltpu
from jax.sharding import PartitionSpec as P

QUERY_HEADS = 16
KEY_VALUE_HEADS = 8
HEAD_SIZE = 128
GROUP = QUERY_HEADS // KEY_VALUE_HEADS
DOCS = 32
BLOCK = 256

epsilon = 1e-06
masked_score = -1e30
scale = HEAD_SIZE ** (-0.5)
half = jnp.bfloat16
f32 = jnp.float32


def inverse_root(value):
    return lax.rsqrt(jnp.mean(value * value, axis=-1, keepdims=True) + epsilon)


def norm_pullback(grad_in, normed_rows, inverse, gain):
    scaled = grad_in * gain
    return inverse * (scaled - normed_rows * jnp.mean(normed_rows * scaled, axis=-1, keepdims=True))


def matrix_product(left, right):
    return jnp.dot(left, right, preferred_element_type=f32)


def outer_sum(left, right):
    return lax.dot_general(left, right, (((0,), (0,)), ((), ())), preferred_element_type=f32)


def through_rows(left, right):
    return lax.dot_general(left, right, (((1,), (1,)), ((), ())), preferred_element_type=f32)


def place_of(block, where_ref, per):
    return ((block // per) ^ where_ref[0]) * per + block % per


def stack_heads(ref, group):
    first = group * GROUP * HEAD_SIZE
    return jnp.concatenate(
        [ref[:, first + h * HEAD_SIZE : first + (h + 1) * HEAD_SIZE] for h in range(GROUP)], axis=0
    )


def stack_columns(ref, first):
    return jnp.concatenate([ref[:, first + h : first + h + 1] for h in range(GROUP)], axis=0)


def allowed_block(start_ref, block, keys):
    rows = lax.broadcasted_iota(jnp.int32, (GROUP * BLOCK, BLOCK), 0)
    spot_query = block * BLOCK + jnp.where(rows >= BLOCK, rows - BLOCK, rows)
    spot_key = keys * BLOCK + lax.broadcasted_iota(jnp.int32, (GROUP * BLOCK, BLOCK), 1)
    start = jnp.concatenate([start_ref[...]] * GROUP, axis=0)
    return (spot_key >= start) & (spot_key <= spot_query)


def attention_forward(where_ref, low_ref, qkva, start, gain_q, gain_k, gated, mixed, log_norm, keys, values, scores, *, groups):
    block = pl.program_id(0)
    q_width = groups * GROUP * HEAD_SIZE
    kv_width = groups * HEAD_SIZE
    here = pl.ds(pl.multiple_of(block * BLOCK, BLOCK), BLOCK)
    for g in range(groups):
        at = slice(g * HEAD_SIZE, (g + 1) * HEAD_SIZE)
        k = qkva[:, q_width + g * HEAD_SIZE : q_width + (g + 1) * HEAD_SIZE]
        keys[here, at] = (k * inverse_root(k) * gain_k[...]).astype(half)
        v = qkva[:, q_width + kv_width + g * HEAD_SIZE : q_width + kv_width + (g + 1) * HEAD_SIZE]
        values[here, at] = v.astype(half)
    low = low_ref[block]
    lane = lax.broadcasted_iota(jnp.int32, (BLOCK, HEAD_SIZE), 1)
    norms = jnp.zeros((BLOCK, HEAD_SIZE), f32)
    for g in range(groups):
        at = slice(g * HEAD_SIZE, (g + 1) * HEAD_SIZE)
        q = stack_heads(qkva, g)
        qn = (q * inverse_root(q) * gain_q[...]).astype(half)

        def score_step(j, peak):
            span = pl.ds(pl.multiple_of(j * BLOCK, BLOCK), BLOCK)
            s = through_rows(qn, keys[span, at]) * scale
            s = jnp.where(allowed_block(start, block, j), s, masked_score)
            scores[:, span] = s
            return jnp.maximum(peak, jnp.max(s, axis=-1, keepdims=True))

        peak = lax.fori_loop(low, block + 1, score_step, jnp.full((GROUP * BLOCK, 1), masked_score, f32))

        def exp_step(j, total):
            span = pl.ds(pl.multiple_of(j * BLOCK, BLOCK), BLOCK)
            e = jnp.exp(scores[:, span] - peak)
            scores[:, span] = e
            return total + jnp.sum(e, axis=-1, keepdims=True)

        total = lax.fori_loop(low, block + 1, exp_step, jnp.zeros((GROUP * BLOCK, 1), f32))

        def mix_step(j, mix):
            span = pl.ds(pl.multiple_of(j * BLOCK, BLOCK), BLOCK)
            p = (scores[:, span] / total).astype(half)
            return mix + matrix_product(p, values[span, at])

        mix = lax.fori_loop(low, block + 1, mix_step, jnp.zeros((GROUP * BLOCK, HEAD_SIZE), f32))
        lse = peak + jnp.log(total)
        for h in range(GROUP):
            head = g * GROUP + h
            to = slice(head * HEAD_SIZE, (head + 1) * HEAD_SIZE)
            o = mix[h * BLOCK : (h + 1) * BLOCK]
            gate = jax.nn.sigmoid(qkva[:, q_width + 2 * kv_width + head : q_width + 2 * kv_width + head + 1])
            mixed[:, to] = o
            gated[:, to] = (o * gate).astype(half)
            norms = jnp.where(lane == head, lse[h * BLOCK : (h + 1) * BLOCK], norms)
    log_norm[...] = norms


def attention_backward(
    where_ref, low_ref, qkva, start, gain_q, gain_k, mixed, log_norm, grad_gated,
    grad_qkva, grad_gains,
    keys, values, raw_keys, grad_keys, grad_values, probs, grad_probs, *, groups, per,
):
    block = pl.program_id(0)
    blocks = pl.num_programs(0)
    q_width = groups * GROUP * HEAD_SIZE
    kv_width = groups * HEAD_SIZE
    here = pl.ds(pl.multiple_of(block * BLOCK, BLOCK), BLOCK)
    out_rows = pl.ds(pl.multiple_of(place_of(block, where_ref, per) * BLOCK, BLOCK), BLOCK)

    @pl.when(block == 0)
    def _():
        grad_gains[...] = jnp.zeros_like(grad_gains)

    for g in range(groups):
        at = slice(g * HEAD_SIZE, (g + 1) * HEAD_SIZE)
        k = qkva[:, q_width + g * HEAD_SIZE : q_width + (g + 1) * HEAD_SIZE]
        raw_keys[here, at] = k
        keys[here, at] = (k * inverse_root(k) * gain_k[...]).astype(half)
        v = qkva[:, q_width + kv_width + g * HEAD_SIZE : q_width + kv_width + (g + 1) * HEAD_SIZE]
        values[here, at] = v.astype(half)
    grad_keys[here, :] = jnp.zeros((BLOCK, kv_width), f32)
    grad_values[here, :] = jnp.zeros((BLOCK, kv_width), f32)
    low = low_ref[block]
    lane = lax.broadcasted_iota(jnp.int32, (BLOCK, HEAD_SIZE), 1)
    grad_logits = jnp.zeros((BLOCK, HEAD_SIZE), f32)
    for g in range(groups):
        at = slice(g * HEAD_SIZE, (g + 1) * HEAD_SIZE)
        q = stack_heads(qkva, g)
        rq = inverse_root(q)
        nq = q * rq
        qn = (nq * gain_q[...]).astype(half)
        lse = stack_columns(log_norm, g * GROUP)
        gate = jax.nn.sigmoid(stack_columns(qkva, q_width + 2 * kv_width + g * GROUP))
        upstream = stack_heads(grad_gated, g).astype(f32)
        o = stack_heads(mixed, g)
        da = jnp.sum(upstream * o, axis=-1, keepdims=True) * gate * (1.0 - gate)
        do = (upstream * gate).astype(half)
        for h in range(GROUP):
            grad_logits = jnp.where(lane == g * GROUP + h, da[h * BLOCK : (h + 1) * BLOCK], grad_logits)

        def prob_step(j, delta):
            span = pl.ds(pl.multiple_of(j * BLOCK, BLOCK), BLOCK)
            s = through_rows(qn, keys[span, at]) * scale
            p = jnp.where(allowed_block(start, block, j), jnp.exp(s - lse), 0.0)
            dp = through_rows(do, values[span, at])
            probs[:, span] = p
            grad_probs[:, span] = dp
            grad_values[span, at] += outer_sum(p.astype(half), do)
            return delta + jnp.sum(p * dp, axis=-1, keepdims=True)

        delta = lax.fori_loop(low, block + 1, prob_step, jnp.zeros((GROUP * BLOCK, 1), f32))

        def score_step(j, dq):
            span = pl.ds(pl.multiple_of(j * BLOCK, BLOCK), BLOCK)
            ds = (probs[:, span] * (grad_probs[:, span] - delta)).astype(half)
            grad_keys[span, at] += outer_sum(ds, qn)
            return dq + matrix_product(ds, keys[span, at])

        dqn = lax.fori_loop(low, block + 1, score_step, jnp.zeros((GROUP * BLOCK, HEAD_SIZE), f32)) * scale
        grad_gains[0:1, :] += jnp.sum(dqn * nq, axis=0, keepdims=True)
        dq = norm_pullback(dqn, nq, rq, gain_q[...]).astype(half)
        for h in range(GROUP):
            head = g * GROUP + h
            grad_qkva[out_rows, head * HEAD_SIZE : (head + 1) * HEAD_SIZE] = dq[h * BLOCK : (h + 1) * BLOCK]
    grad_qkva[out_rows, q_width + 2 * kv_width :] = grad_logits.astype(half)

    @pl.when(block == blocks - 1)
    def _():
        def finish(j, carry):
            span = pl.ds(pl.multiple_of(j * BLOCK, BLOCK), BLOCK)
            rows = pl.ds(pl.multiple_of(place_of(j, where_ref, per) * BLOCK, BLOCK), BLOCK)
            for g in range(groups):
                at = slice(g * HEAD_SIZE, (g + 1) * HEAD_SIZE)
                k = raw_keys[span, at]
                rk = inverse_root(k)
                nk = k * rk
                dkn = grad_keys[span, at] * scale
                grad_gains[1:2, :] += jnp.sum(dkn * nk, axis=0, keepdims=True)
                dk = norm_pullback(dkn, nk, rk, gain_k[...]).astype(half)
                grad_qkva[rows, q_width + g * HEAD_SIZE : q_width + (g + 1) * HEAD_SIZE] = dk
                grad_qkva[rows, q_width + kv_width + g * HEAD_SIZE : q_width + kv_width + (g + 1) * HEAD_SIZE] = (
                    grad_values[span, at].astype(half)
                )
            return carry

        lax.fori_loop(0, blocks, finish, 0)


def run_attention_forward(qkva, start, low, where, gain_q, gain_k, per):
    length, width = qkva.shape
    groups = (width - HEAD_SIZE) // ((GROUP + 2) * HEAD_SIZE)
    q_width = groups * GROUP * HEAD_SIZE
    kv_width = groups * HEAD_SIZE

    def rows(i, where_ref, low_ref):
        return (place_of(i, where_ref, per), 0)

    def whole(i, where_ref, low_ref):
        return (0, 0)

    def body(*refs):
        attention_forward(*refs, groups=groups)

    pairs = length * length // 2
    return pl.pallas_call(
        body,
        grid_spec=pltpu.PrefetchScalarGridSpec(
            num_scalar_prefetch=2,
            grid=(length // BLOCK,),
            in_specs=[
                pl.BlockSpec((BLOCK, width), rows),
                pl.BlockSpec((BLOCK, 1), lambda i, where_ref, low_ref: (i, 0)),
                pl.BlockSpec((1, HEAD_SIZE), whole),
                pl.BlockSpec((1, HEAD_SIZE), whole),
            ],
            out_specs=[
                pl.BlockSpec((BLOCK, q_width), rows),
                pl.BlockSpec((BLOCK, q_width), rows),
                pl.BlockSpec((BLOCK, HEAD_SIZE), rows),
            ],
            scratch_shapes=[
                pltpu.VMEM((length, kv_width), half),
                pltpu.VMEM((length, kv_width), half),
                pltpu.VMEM((GROUP * BLOCK, length), f32),
            ],
        ),
        out_shape=(
            jax.ShapeDtypeStruct((length, q_width), half),
            jax.ShapeDtypeStruct((length, q_width), f32),
            jax.ShapeDtypeStruct((length, HEAD_SIZE), f32),
        ),
        cost_estimate=pl.CostEstimate(
            flops=pairs * q_width * 2, bytes_accessed=length * (width + q_width) * 4, transcendentals=pairs * groups
        ),
        name="attention_forward",
    )(where, low, qkva, start, gain_q, gain_k)


def run_attention_backward(qkva, start, low, where, gain_q, gain_k, mixed, log_norm, grad_gated, per):
    length, width = qkva.shape
    groups = (width - HEAD_SIZE) // ((GROUP + 2) * HEAD_SIZE)
    q_width = groups * GROUP * HEAD_SIZE
    kv_width = groups * HEAD_SIZE

    def rows(i, where_ref, low_ref):
        return (place_of(i, where_ref, per), 0)

    def whole(i, where_ref, low_ref):
        return (0, 0)

    def body(*refs):
        attention_backward(*refs, groups=groups, per=per)

    pairs = length * length // 2
    return pl.pallas_call(
        body,
        grid_spec=pltpu.PrefetchScalarGridSpec(
            num_scalar_prefetch=2,
            grid=(length // BLOCK,),
            in_specs=[
                pl.BlockSpec((BLOCK, width), rows),
                pl.BlockSpec((BLOCK, 1), lambda i, where_ref, low_ref: (i, 0)),
                pl.BlockSpec((1, HEAD_SIZE), whole),
                pl.BlockSpec((1, HEAD_SIZE), whole),
                pl.BlockSpec((BLOCK, q_width), rows),
                pl.BlockSpec((BLOCK, HEAD_SIZE), rows),
                pl.BlockSpec((BLOCK, q_width), rows),
            ],
            out_specs=[
                pl.BlockSpec((length, width), whole),
                pl.BlockSpec((8, HEAD_SIZE), whole),
            ],
            scratch_shapes=[
                pltpu.VMEM((length, kv_width), half),
                pltpu.VMEM((length, kv_width), half),
                pltpu.VMEM((length, kv_width), f32),
                pltpu.VMEM((length, kv_width), f32),
                pltpu.VMEM((length, kv_width), f32),
                pltpu.VMEM((GROUP * BLOCK, length), f32),
                pltpu.VMEM((GROUP * BLOCK, length), f32),
            ],
        ),
        out_shape=(
            jax.ShapeDtypeStruct((length, width), half),
            jax.ShapeDtypeStruct((8, HEAD_SIZE), f32),
        ),
        cost_estimate=pl.CostEstimate(
            flops=pairs * q_width * 5, bytes_accessed=length * (width + q_width) * 6, transcendentals=pairs * groups
        ),
        name="attention_backward",
    )(where, low, qkva, start, gain_q, gain_k, mixed, log_norm, grad_gated)


def after(x, *others):
    return lax.optimization_barrier((x,) + others)[0]


def build(rep_size, dp_size, ctx_size):
    R, D, C = rep_size, dp_size, ctx_size
    pair = D == 2
    spread = D if KEY_VALUE_HEADS % (D * C) == 0 else 1
    groups = KEY_VALUE_HEADS // C
    q_width = groups * GROUP * HEAD_SIZE
    kv_width = groups * HEAD_SIZE

    def hop(x, k):
        if k == 0:
            return x
        return lax.ppermute(x, "ctx", [(i, i ^ k) for i in range(C)])

    def other_dp(x):
        return lax.ppermute(x, "dp", [(i, 1 - i) for i in range(2)])

    def gather_blocks(x):
        far = hop(x, 2)
        return [x, hop(x, 1), far, hop(far, 1)]

    def scatter_blocks(near, far):
        rows = near.shape[0] // 2
        cross = hop(far[rows:].astype(half), 1)
        across = hop((far[:rows] + cross.astype(f32)).astype(half), 2)
        beside = hop(near[rows:].astype(half), 1)
        return near[:rows] + beside.astype(f32) + across.astype(f32)

    def total_over(x):
        for k in (1, 2):
            x = x + hop(x, k)
        x = x + other_dp(x) if pair else lax.psum(x, "dp")
        if R == 4:
            for k in (1, 2):
                x = x + lax.ppermute(x, "rep", [(i, i ^ k) for i in range(R)])
            return x
        return lax.psum(x, "rep")

    def body(
        hidden_in, segments, cotangent, attn_gain, w_query, key_projection, value_projection,
        q_gain, k_gain, w_gate, w_out, mlp_gain, w_gate_ff, w_up, w_down,
    ):
        sequences, rows, model = hidden_in.shape
        assert sequences == 1 and C == 4
        length = rows * C
        dp = lax.axis_index("dp")
        ctx = lax.axis_index("ctx")
        part = attn_gain.shape[0]
        hp = q_gain.shape[0]
        units = w_down.shape[0]

        def at_row(x, first, count):
            return lax.dynamic_slice_in_dim(x, first, count, axis=0)

        def at_column(x, first, count):
            return lax.dynamic_slice_in_dim(x, first, count, axis=1)

        def put_row(buffer, x, first):
            return lax.dynamic_update_slice_in_dim(buffer, x, first, axis=0)

        def put_column(buffer, x, first):
            return lax.dynamic_update_slice_in_dim(buffer, x, first, axis=1)

        def first_mine(x):
            m = x.shape[0] // 2
            return jnp.where(dp == 0, x, jnp.concatenate([x[m:], x[:m]], axis=0))

        def head_columns(w, per_head, c):
            w = w.reshape(part, spread, C, -1)
            return lax.dynamic_index_in_dim(w, c, axis=2, keepdims=False).reshape(part, groups * per_head)

        def unit_columns(w, c):
            w = w.reshape(part, D, C, units)
            return lax.dynamic_index_in_dim(w, c, axis=2, keepdims=False).reshape(part, D * units)

        def gather_rows(blocks):
            width = blocks[0].shape[1]
            got = [hop(b, k) for k, b in enumerate(blocks)]
            if not pair:
                mine = jnp.zeros((C * part, width), half)
                for k in range(C):
                    mine = put_row(mine, got[k], (ctx ^ k) * part)
                return lax.all_gather(mine, "dp", axis=0, tiled=True), got
            whole = jnp.zeros((D * C * part, width), half)
            away = [other_dp(b) for b in got]
            for k in range(C):
                whole = put_row(whole, got[k], (dp * C + (ctx ^ k)) * part)
                whole = put_row(whole, away[k], ((1 - dp) * C + (ctx ^ k)) * part)
            return whole, got

        def split_product(left_near, left_far, right_near, right_far):
            count = left_near.shape[1] // D
            if not pair:
                grad = outer_sum(left_near, right_near) + outer_sum(left_far, right_far)
                return lax.psum_scatter(grad.astype(half), "dp", scatter_dimension=0, tiled=True)
            other, own = (1 - dp) * count, dp * count
            away = outer_sum(at_column(left_near, other, count), right_near) + outer_sum(
                at_column(left_far, other, count), right_far
            )
            away = other_dp(away.astype(half))
            mine = outer_sum(at_column(left_near, own, count), right_near) + outer_sum(
                at_column(left_far, own, count), right_far
            )
            return (mine + away.astype(f32)).astype(half)

        def return_rows(total):
            return [hop(at_row(total, (ctx ^ k) * part, part), k) for k in range(C)]

        small = jnp.concatenate([attn_gain, mlp_gain, q_gain, k_gain, segments[0].astype(f32)]).astype(half)
        small = lax.all_gather(small, ("dp", "ctx"), axis=0, tiled=False)
        ready = small
        small = small.astype(f32)
        gain_a = small[:, :part].reshape(1, -1)
        gain_m = small[:, part : 2 * part].reshape(1, -1)
        gain_q = small[:, 2 * part : 2 * part + hp].reshape(1, -1)
        gain_k = small[:, 2 * part + hp : 2 * part + 2 * hp].reshape(1, -1)
        seq_segments = at_row(small[:, 2 * part + 2 * hp :], dp * C, C).reshape(-1)

        doc = lax.broadcasted_iota(jnp.int32, (DOCS, 1), 0).astype(f32)
        live = seq_segments >= 0
        before = jnp.sum(jnp.where(live[None, :] & (seq_segments[None, :] < doc), 1.0, 0.0), axis=1)
        start_of = jnp.sum(jnp.where(seq_segments[:, None] == doc[:, 0][None, :], before[None, :], 0.0), axis=1)
        spot = lax.broadcasted_iota(jnp.int32, (length,), 0)
        start = jnp.where(live, start_of.astype(jnp.int32), spot)
        low = start[::BLOCK] // BLOCK
        start = start[:, None]
        where = ctx.reshape(1).astype(jnp.int32)

        pad = HEAD_SIZE - groups * GROUP
        attn_blocks = [
            jnp.concatenate(
                [
                    head_columns(w_query, GROUP * HEAD_SIZE, ctx ^ k),
                    head_columns(key_projection, HEAD_SIZE, ctx ^ k),
                    head_columns(value_projection, HEAD_SIZE, ctx ^ k),
                    jnp.pad(head_columns(w_gate, GROUP, ctx ^ k), ((0, 0), (0, pad))),
                ],
                axis=1,
            ).astype(half)
            for k in range(C)
        ]
        w_qkva, attn_got = gather_rows([after(b, ready) for b in attn_blocks])
        x_own = hidden_in[0]
        x_blocks = gather_blocks(after(x_own, ready))
        x_all = jnp.concatenate(x_blocks, axis=0).astype(f32)
        hn = (x_all * inverse_root(x_all) * gain_a).astype(half)

        w_gate_ff_all, gate_got = gather_rows(
            [after(unit_columns(w_gate_ff, ctx ^ k).astype(half), x_blocks[2]) for k in range(C)]
        )
        w_out_half = after(w_out.astype(half), ready)
        if spread == D and pair:
            w_out_mine = first_mine(jnp.concatenate([w_out_half, other_dp(w_out_half)], axis=0))
            w_out_all = jnp.concatenate(gather_blocks(after(w_out_mine, hn)), axis=0)
        else:
            w_out_full = lax.all_gather(w_out_half, ("dp", "ctx"), axis=0, tiled=True)
            span = w_out_full.shape[0] // C
            w_out_all = jnp.concatenate([at_row(w_out_full, (ctx ^ k) * span, span) for k in range(C)], axis=0)

        qkva = matrix_product(hn, w_qkva)
        w_down_half = after(w_down.astype(half), qkva)
        if pair:
            w_down_all = first_mine(jnp.concatenate([w_down_half, other_dp(w_down_half)], axis=0))
        else:
            w_down_all = lax.all_gather(w_down_half, "dp", axis=0, tiled=True)
        gated, mixed, log_norm = run_attention_forward(
            qkva, start, low, where, gain_q, gain_k, rows // BLOCK
        )
        w_up_all, up_got = gather_rows([after(unit_columns(w_up, ctx ^ k).astype(half), gated) for k in range(C)])
        gated_own = jnp.concatenate(
            [hop(gated[k * rows : (k + 1) * rows], k) for k in range(C)], axis=1
        )
        x_f = x_own.astype(f32)
        x1 = x_f + matrix_product(gated_own, w_out_all)
        inverse_m = inverse_root(x1)
        nm = x1 * inverse_m
        hm_own = (nm * gain_m).astype(half)
        hm = gather_blocks(hm_own)
        hm = (jnp.concatenate(hm[:2], axis=0), jnp.concatenate(hm[2:], axis=0))

        valid = (segments.reshape(rows, 1) >= 0).astype(f32)
        dy_own = cotangent[0].astype(f32) * valid
        dy = gather_blocks(after(dy_own.astype(half), hm_own))
        dy = (jnp.concatenate(dy[:2], axis=0), jnp.concatenate(dy[2:], axis=0))

        hidden, grad_gate_half, grad_up_half = [], [], []
        for rows_m, rows_dy in zip(hm, dy):
            gate_ff = matrix_product(rows_m, w_gate_ff_all)
            up_ff = matrix_product(rows_m, w_up_all)
            grad_hidden = through_rows(rows_dy, w_down_all)
            sig = jax.nn.sigmoid(gate_ff)
            hidden.append((gate_ff * sig * up_ff).astype(half))
            grad_gate_half.append((grad_hidden * up_ff * sig * (1.0 + gate_ff * (1.0 - sig))).astype(half))
            grad_up_half.append((grad_hidden * gate_ff * sig).astype(half))
        dhm_parts = [
            through_rows(a, w_gate_ff_all) + through_rows(b, w_up_all)
            for a, b in zip(grad_gate_half, grad_up_half)
        ]
        dhm = scatter_blocks(*dhm_parts)
        grad_gm = jnp.sum(dhm * nm, axis=0)
        dx1 = dy_own + norm_pullback(dhm, nm, inverse_m, gain_m)
        dx1_half = dx1.astype(half)

        grad_down = split_product(hidden[0], hidden[1], dy[0], dy[1])
        grad_down = lax.psum(grad_down, "rep")
        grad_gate_ff = split_product(hm[0], hm[1], grad_gate_half[0], grad_gate_half[1])
        grad_gate_ff = lax.psum(after(grad_gate_ff, grad_down), "rep")
        grad_up = split_product(hm[0], hm[1], grad_up_half[0], grad_up_half[1])
        grad_up = lax.psum(after(grad_up, grad_gate_ff), "rep")

        y = scatter_blocks(*[matrix_product(h, w_down_all) for h in hidden])
        layer_out = (x1 + y).astype(half)[None]

        grad_gated_own = through_rows(dx1_half, w_out_all).astype(half)
        grad_gated = jnp.concatenate(
            [hop(grad_gated_own[:, k * q_width : (k + 1) * q_width], k) for k in range(C)], axis=0
        )
        dx1_blocks = gather_blocks(after(dx1_half, grad_gated_own))
        dx1_near, dx1_far = jnp.concatenate(dx1_blocks[:2], axis=0), jnp.concatenate(dx1_blocks[2:], axis=0)
        gated_near, gated_far = gated[: 2 * rows], gated[2 * rows :]
        if spread == D and pair:
            grad_out = split_product(gated_near, gated_far, dx1_near, dx1_far)
        else:
            grad_out = outer_sum(gated_near, dx1_near) + outer_sum(gated_far, dx1_far)
            grad_out = put_row(jnp.zeros((model, model), half), grad_out.astype(half), ctx * grad_out.shape[0])
            grad_out = lax.psum_scatter(grad_out, ("dp", "ctx"), scatter_dimension=0, tiled=True)
        grad_out = lax.psum(after(grad_out, grad_up), "rep")

        grad_qkva, grad_gains = run_attention_backward(
            qkva, start, low, where, gain_q, gain_k, mixed, log_norm, grad_gated, rows // BLOCK
        )
        grad_attn = split_product(hn[: 2 * rows], hn[2 * rows :], grad_qkva[: 2 * rows], grad_qkva[2 * rows :])
        grad_attn = lax.psum(after(grad_attn, grad_out), "rep")
        dhn = scatter_blocks(
            through_rows(grad_qkva[: 2 * rows], w_qkva), through_rows(grad_qkva[2 * rows :], w_qkva)
        )
        inverse_a = inverse_root(x_f)
        na = x_f * inverse_a
        grad_ga = jnp.sum(dhn * na, axis=0)
        input_grad = (dx1 + norm_pullback(dhn, na, inverse_a, gain_a)).astype(half)[None]

        def unit_grad(total):
            out = jnp.zeros((part, D * C * units), f32)
            for k, b in enumerate(return_rows(total)):
                for d in range(D):
                    piece = b[:, d * units : (d + 1) * units].astype(f32)
                    out = put_column(out, piece, (d * C + (ctx ^ k)) * units)
            return out

        attn_back = return_rows(grad_attn)

        def head_grad(first, width):
            per = width // spread
            out = jnp.zeros((part, C * width), f32)
            for k, b in enumerate(attn_back):
                for d in range(spread):
                    piece = b[:, first + d * per : first + (d + 1) * per].astype(f32)
                    out = put_column(out, piece, (d * C + (ctx ^ k)) * per)
            return out

        gains = total_over(jnp.concatenate([grad_ga, grad_gm, grad_gains[0], grad_gains[1]]).reshape(-1, HEAD_SIZE))
        gains = gains.reshape(-1)
        at = dp * C + ctx
        return (
            layer_out,
            input_grad,
            at_row(gains, at * part, part),
            head_grad(0, q_width),
            head_grad(q_width, kv_width),
            head_grad(q_width + kv_width, kv_width),
            at_row(gains, 2 * model + at * hp, hp),
            at_row(gains, 2 * model + HEAD_SIZE + at * hp, hp),
            head_grad(q_width + 2 * kv_width, groups * GROUP),
            grad_out.astype(f32),
            at_row(gains, model + at * part, part),
            unit_grad(grad_gate_ff),
            unit_grad(grad_up),
            grad_down.astype(f32),
        )

    return body


def solution(mesh):
    tokens = P(("rep", "dp"), "ctx", None)
    vector = P(("dp", "ctx"))
    matrix = P(("dp", "ctx"), None)
    weights = (vector, matrix, matrix, matrix, vector, vector, matrix, matrix, vector, matrix, matrix, matrix)
    return jax.shard_map(
        build(mesh.shape["rep"], mesh.shape["dp"], mesh.shape["ctx"]),
        mesh=mesh,
        in_specs=(tokens, P(("rep", "dp"), "ctx"), tokens) + weights,
        out_specs=(tokens, tokens) + weights,
        check_vma=False,
    )
```
